32 devices in a mesh: group: 2 (over y), tile: 4 (over x, core), seq: 4 (over z).
Axes of the slice: x: 2, y: 2, z: 4, core: 2. Of those that a mesh axis runs over, the one named last changes fastest.
Arguments:
- hidden: bfloat16 [8, 1024, 3072], P(('group', 'tile'), 'seq'), parts along dimension 0
- modulation: float32 [10, 3072], P('group'), parts along dimension 0, may hold values from -3 to 3
- w_qkv: bfloat16 [3072, 9216], P('tile', 'seq')
- w_out: bfloat16 [3072, 3072], P('seq', 'tile'), may hold values from -0.109375 to 0.109375
- w_head: bfloat16 [3072, 64], replicated, may hold values from -0.109375 to 0.109375
- latent: float32 [8, 1024, 64], P(('group', 'tile'), 'seq'), parts along dimension 0, may hold values from -6 to 6
- weights_int: int32 [8, 1024], P(('group', 'tile'), 'seq'), parts along dimension 0, may hold values from 1 to 8
- step_index: int32 [2], P('group'), parts along dimension 0, may hold values from 0 to 13
Outputs:
- stepped: float32 [8, 1024, 64], P(('group', 'tile'), 'seq'), parts along dimension 0
- clean: float32 [8, 1024, 64], P(('group', 'tile'), 'seq'), parts along dimension 0
The draws below stay inside these ranges and needn't reach their ends.
There are 2 independent parts, one for each index of `group`. The reference program is written for one: setup_inputs(seed, part) draws one part's arguments, and reference() takes and returns one part's arrays. A program takes and returns all parts, laid end to end along the dimension named above; an argument that names none is the same for every part. Nothing has to cross between parts.
All inputs are finite; a program needn't handle non-finite values.
Results may differ from the reference program's by a relative error of at most 0.0055.
Values may be sent and summed in bfloat16 or wider, within the bound.
A program may use at most 64 MiB of HBM per device.

```python
import math
import jax
import jax.numpy as jnp
from jax import lax

D = 3072
HEADS = 24
HD = 128
C = 64
TILE_LEN = 1024
NSTEPS = 28
TILES = 4
STRIDE = 512
N_SEQ = 4


def draw_hidden(key, part):
    first = jax.random.fold_in(key, 0)
    second = jax.random.fold_in(key, 1)
    third = jax.random.fold_in(key, 2)
    fifth = jax.random.fold_in(key, 4)
    sixth = jax.random.fold_in(key, 5)
    clusters = 16
    rows = jnp.exp(jax.random.uniform(second, (TILES, TILE_LEN, 1), jnp.float32, math.log(0.3), math.log(3.0)))
    cols = jnp.exp(jax.random.uniform(third, (1, 1, D), jnp.float32, math.log(0.3), math.log(3.0)))
    labels = jax.random.randint(fifth, (TILES, TILE_LEN, 1), 0, clusters)
    centres = jax.random.normal(sixth, (TILES, clusters, D), jnp.float32)
    noise = jax.random.normal(first, (TILES, TILE_LEN, D), jnp.float32)
    picked = jnp.take_along_axis(centres, labels, axis=1)
    base = 0.9 * picked + 0.45 * noise
    base = jnp.clip(base, -5.0, 5.0)
    return (base * rows * cols).astype(jnp.bfloat16)


def draw_w_qkv(key, part):
    first, second = jax.random.split(jax.random.fold_in(key, 17), 2)
    scale = 1.0 / math.sqrt(D)
    base = jax.random.normal(first, (D, HEADS, 3, HD), jnp.float32) * scale
    extra = jax.random.normal(second, (D, HEADS, HD), jnp.float32) * scale
    keys = 0.6 * base[:, :, 0] + 0.8 * extra
    stacked = jnp.stack([base[:, :, 0], keys, base[:, :, 2]], axis=2)
    return stacked.reshape(D, 3 * D).astype(jnp.bfloat16)


def set_ends(values, stream_key, least, top_value):
    dims = values.shape
    index_at = [jax.random.randint(jax.random.fold_in(stream_key, axis), (), 0, dims[axis]) for axis in range(len(dims))]
    values = values.at[tuple(index_at)].set(least)
    longest = dims.index(max(dims))
    index_at[longest] = (index_at[longest] + 1) % dims[longest]
    return values.at[tuple(index_at)].set(top_value)


def level_of(key, extent, cuts, least, top_value):
    def one(axis_at, blocks):
        steps = jax.random.uniform(jax.random.fold_in(jax.random.fold_in(key, 6), axis_at), (blocks,), jnp.float32, least / len(cuts), top_value / len(cuts))
        return jnp.repeat(jnp.exp(steps), extent[axis_at] // blocks).reshape((-1,) + (1,) * (len(extent) - axis_at - 1))

    gain = one(*cuts[0])
    for cut in cuts[1:]:
        gain = gain * one(*cut)
    return gain


def normal_values(own_key, dims, width, most, pieces=(), held_as=jnp.bfloat16):
    result = width * jax.random.normal(own_key, dims, jnp.float32)
    if pieces:
        result = result * level_of(own_key, dims, pieces, -0.22, 0.18)
    return jnp.clip(result, -most, most).astype(held_as)


def setup_inputs(seed: int = 0, part: int = 0) -> dict:
    streams_of = jax.random.split(jax.random.key(seed), 9)
    part_splits = jax.random.split(jax.random.fold_in(streams_of[8], part), 9)
    return {
        "hidden": draw_hidden(jax.random.fold_in(jax.random.fold_in(streams_of[8], part), 71), part),
        "modulation": normal_values(part_splits[1], (5, D), 0.5, 3.0, (), jnp.float32),
        "w_qkv": draw_w_qkv(jax.random.fold_in(streams_of[8], 71), part),
        "w_out": normal_values(streams_of[3], (D, D), D ** -0.5, 0.109375, ((0, 4), (1, 4))),
        "w_head": normal_values(streams_of[4], (D, C), D ** -0.5, 0.109375),
        "latent": normal_values(part_splits[5], (TILES, TILE_LEN, C), 1.0, 6.0, ((0, 4), (1, 4)), jnp.float32),
        "weights_int": set_ends(jax.random.randint(part_splits[6], (TILES, TILE_LEN), 1, 9), jax.random.fold_in(part_splits[6], 1), 1, 8).astype(jnp.int32),
        "step_index": jax.random.randint(part_splits[7], (1,), 0, NSTEPS // 2).astype(jnp.int32),
    }


def layer_norm(values):
    mean = lax.optimization_barrier(jnp.mean(values, axis=-1, keepdims=True))
    centred = values - mean
    spread = lax.optimization_barrier(jnp.mean(centred * centred, axis=-1, keepdims=True))
    return centred * lax.rsqrt(spread + 1e-06)

def root_norm(values):
    return values * lax.rsqrt(lax.optimization_barrier(jnp.mean(values * values, axis=-1, keepdims=True)) + 1e-06)

def noise_level(index, steps):
    level = 1.0 - index / steps
    return 3.0 * level / (1.0 + 2.0 * level)

def reference(hidden, modulation, w_qkv, w_out, w_head, latent, weights_int, step_index):
    qkv_full = w_qkv.astype(jnp.float32)
    out_groups = w_out.astype(jnp.float32).reshape(N_SEQ, D // N_SEQ, D)
    head_full = w_head.astype(jnp.float32)

    def one_tile(tokens):
        local = tokens.astype(jnp.float32)
        norm_in = (layer_norm(local) * (1.0 + modulation[1]) + modulation[0]).astype(jnp.bfloat16)
        proj = jnp.dot(norm_in.astype(jnp.float32), qkv_full)
        proj = proj.reshape(TILE_LEN, HEADS, 3, HD)
        queries = root_norm(proj[:, :, 0]).astype(jnp.bfloat16).astype(jnp.float32)
        keys = root_norm(proj[:, :, 1]).astype(jnp.bfloat16).astype(jnp.float32)
        values = proj[:, :, 2].astype(jnp.bfloat16).astype(jnp.float32)
        scores = jnp.einsum('qhe,khe->hqk', queries, keys) / math.sqrt(HD)
        expo = jnp.exp(scores)
        probs = (expo / lax.optimization_barrier(jnp.sum(expo, axis=-1, keepdims=True))).astype(jnp.bfloat16).astype(jnp.float32)
        attended = jnp.einsum('hqk,khe->qhe', probs, values).astype(jnp.bfloat16)
        attended = attended.astype(jnp.float32).reshape(TILE_LEN, N_SEQ, D // N_SEQ)
        parts = jnp.einsum('lgd,gdo->glo', attended, out_groups).astype(jnp.bfloat16)
        summed = lax.optimization_barrier(jnp.sum(parts.astype(jnp.float32), axis=0))
        mixed = local + modulation[2] * summed
        norm_out = (layer_norm(mixed) * (1.0 + modulation[4]) + modulation[3]).astype(jnp.bfloat16)
        return jnp.dot(norm_out.astype(jnp.float32), head_full)
    velocity = lax.map(one_tile, hidden)
    index = step_index[0].astype(jnp.float32)
    now = noise_level(index, NSTEPS)
    after = noise_level(index + 1.0, NSTEPS)
    moved = latent + (after - now) * velocity
    guess = latent - now * velocity
    weight = weights_int.astype(jnp.float32)
    band = (TILES - 1) * STRIDE + TILE_LEN
    places = (jnp.arange(TILES, dtype=jnp.int32)[:, None] * STRIDE + jnp.arange(TILE_LEN, dtype=jnp.int32)[None, :]).reshape(-1)
    stacked = jnp.concatenate([moved, guess], axis=2) * weight[:, :, None]
    totals = jnp.zeros((band, 2 * C), jnp.float32).at[places].add(stacked.reshape(-1, 2 * C))
    norms = jnp.zeros((band,), jnp.float32).at[places].add(weight.reshape(-1))
    joined = (totals[places] / norms[places][:, None]).reshape(TILES, TILE_LEN, 2 * C)
    return (joined[:, :, :C], joined[:, :, C:])
```

```python
import functools
import math

import jax
import jax.numpy as jnp
from jax import lax
from jax.experimental import pallas as pl
from jax.experimental.pallas import tpu as pltpu
from jax.sharding import PartitionSpec as P

HD = 128
NSTEPS = 28


def layer_norm(values):
    mean = jnp.mean(values, axis=-1, keepdims=True)
    centred = values - mean
    spread = jnp.mean(centred * centred, axis=-1, keepdims=True)
    return centred * lax.rsqrt(spread + 1e-06)


def root_norm(values):
    return values * lax.rsqrt(jnp.mean(values * values, axis=-1, keepdims=True) + 1e-06)


def noise_level(index, steps):
    level = 1.0 - index / steps
    return 3.0 * level / (1.0 + 2.0 * level)


MESH = pl.DeviceIdType.MESH


def run(cond, body):
    if cond is None:
        body()
    else:
        pl.when(cond)(body)


def arrives(place, count, way, far):
    return place >= far if way == 0 else place <= count - 1 - far


def goes_on(place, count, way):
    return place < count - 1 if way == 0 else place > 0


def gather_kernel(
    groups, chips, seqs, norm, wq, wo, n_all, q_all, o_all, v_norm, v_wq, v_wo, local,
    nz_s, nz_r, oz_s, oz_r, qx_s, qx_r, ox_s, ox_r, qy_s, qy_r, oy_s, oy_r, qc_s, qc_r, oc_s, oc_r,
):
    group, tile, place = lax.axis_index("group"), lax.axis_index("tile"), lax.axis_index("seq")
    chip, core = tile // 2, tile % 2
    other = 1 - core
    partner = {"tile": chip * 2 + other}
    q_rows, o_rows = wq.shape[0] // groups, wo.shape[0] // groups
    both = jnp.logical_and

    def q_part(owner, part):
        return q_all.at[owner, pl.ds(pl.multiple_of(part * q_rows, 8), q_rows)]

    def o_part(owner, row, part):
        return o_all.at[owner, row, pl.ds(pl.multiple_of(part * o_rows, 8), o_rows)]

    def along_seq(way):
        return {"seq": place + 1 - 2 * way}

    def along_chip(way):
        return {"tile": tile + 2 - 4 * way}

    def peer(step):
        return {"group": (group + step) % groups}

    barrier = pltpu.get_barrier_semaphore()
    greet = [(goes_on(place, seqs, way), along_seq(way)) for way in (0, 1)]
    greet += [(goes_on(chip, chips, way), along_chip(way)) for way in (0, 1)]
    greet += [(None, peer(step)) for step in range(1, groups)] + [(None, partner)]
    for cond, device in greet:
        run(cond, lambda device=device: pl.semaphore_signal(barrier, inc=1, device_id=device, device_id_type=MESH))
    met = groups + sum(goes_on(at, count, way).astype(jnp.int32) for at, count in ((place, seqs), (chip, chips)) for way in (0, 1))
    pl.semaphore_wait(barrier, met)

    sent = []

    def copy(source, target, send, recv, device):
        return pltpu.make_async_remote_copy(
            src_ref=source, dst_ref=target, send_sem=send, recv_sem=recv, device_id=device, device_id_type=MESH
        )

    def start(cond, *made):
        run(cond, lambda: copy(*made).start())
        sent.append((cond, made))

    def arrived(cond, target, send, recv, device):
        run(cond, lambda: copy(target, target, send, recv, device).wait_recv())

    def q_to_peers(cond, at, source):
        for step in range(1, groups):
            start(cond, source, q_part(at * 2 + core, group), qy_s.at[at, step], qy_r.at[at, step], peer(step))

    def q_to_partner(cond, at, part, source):
        start(cond, source, q_part(at * 2 + core, part), qc_s.at[at, part], qc_r.at[at, part], partner)

    def o_to_peers(cond, at, row, source):
        for step in range(1, groups):
            start(cond, source, o_part(at * 2 + core, row, group), oy_s.at[at, row, step], oy_r.at[at, row, step], peer(step))

    def o_to_partner(cond, at, row, part, source):
        start(cond, source, o_part(at * 2 + core, row, part), oc_s.at[at, row, part], oc_r.at[at, row, part], partner)

    def o_along_chip(cond, way, far, at, row, source):
        start(cond, source, o_part(at * 2 + core, row, group), ox_s.at[way, far, row], ox_r.at[way, far, row], along_chip(way))

    loads = [pltpu.make_async_copy(a, b, local.at[k]) for k, (a, b) in enumerate(((norm, v_norm), (wq, v_wq), (wo, v_wo)))]
    for load in loads:
        load.start()

    own_q = wq.at[pl.ds(pl.multiple_of(group * q_rows, 8), q_rows)]
    own_o = wo.at[pl.ds(pl.multiple_of(group * o_rows, 8), o_rows)]
    for way in (0, 1):
        go = goes_on(place, seqs, way)
        start(go, own_o, o_part(tile, place, group), oz_s.at[way, 1], oz_r.at[way, 1], along_seq(way))
        start(go, norm, n_all.at[place], nz_s.at[way, 1], nz_r.at[way, 1], along_seq(way))
        go = goes_on(chip, chips, way)
        start(go, own_q, q_part(tile, group), qx_s.at[way, 1], qx_r.at[way, 1], along_chip(way))
        o_along_chip(go, way, 1, chip, place, own_o)
    for part in range(groups):
        q_to_partner(None, chip, part, wq.at[pl.ds(part * q_rows, q_rows)])
        o_to_partner(None, chip, place, part, wo.at[pl.ds(part * o_rows, o_rows)])

    stores = [pltpu.make_async_copy(b, a, local.at[k]) for k, (a, b) in enumerate(((n_all.at[place], v_norm), (q_all.at[tile], v_wq), (o_all.at[tile, place], v_wo)))]
    for load in loads:
        load.wait()
    for store in stores:
        store.start()

    def seq_step(far):
        for way in (0, 1):
            here = arrives(place, seqs, way, far)
            row = place - far if way == 0 else place + far
            piece = o_part(tile, row, group)
            arrived(here, piece, oz_s.at[way, far], oz_r.at[way, far], along_seq(way))
            if far < seqs - 1:
                start(both(here, goes_on(place, seqs, way)), piece, piece, oz_s.at[way, far + 1], oz_r.at[way, far + 1], along_seq(way))
            for side in (0, 1):
                o_along_chip(both(here, goes_on(chip, chips, side)), side, 1, chip, row, piece)
            o_to_peers(here, chip, row, piece)
            o_to_partner(here, chip, row, group, piece)
        for way in (0, 1):
            here = arrives(place, seqs, way, far)
            row = place - far if way == 0 else place + far
            piece = n_all.at[row]
            arrived(here, piece, nz_s.at[way, far], nz_r.at[way, far], along_seq(way))
            if far < seqs - 1:
                start(both(here, goes_on(place, seqs, way)), piece, piece, nz_s.at[way, far + 1], nz_r.at[way, far + 1], along_seq(way))

    def chip_step(far):
        for way in (0, 1):
            here = arrives(chip, chips, way, far)
            at = chip - far if way == 0 else chip + far
            piece = q_part(at * 2 + core, group)
            arrived(here, piece, qx_s.at[way, far], qx_r.at[way, far], along_chip(way))
            if far < chips - 1:
                start(both(here, goes_on(chip, chips, way)), piece, piece, qx_s.at[way, far + 1], qx_r.at[way, far + 1], along_chip(way))
            q_to_peers(here, at, piece)
            q_to_partner(here, at, group, piece)

    for far in range(1, max(chips, seqs)):
        if far < seqs:
            seq_step(far)
        if far < chips:
            chip_step(far)

    for far in range(1, chips):
        for way in (0, 1):
            here = arrives(chip, chips, way, far)
            at = chip - far if way == 0 else chip + far

            for row in range(seqs):
                piece = o_part(at * 2 + core, row, group)
                arrived(here, piece, ox_s.at[way, far, row], ox_r.at[way, far, row], along_chip(way))
                if far < chips - 1:
                    o_along_chip(both(here, goes_on(chip, chips, way)), way, far + 1, at, row, piece)
                o_to_peers(here, at, row, piece)
                o_to_partner(here, at, row, group, piece)

    for step in range(1, groups):
        part = (group + groups - step) % groups
        for at in range(chips):
            away = chip != at
            piece = q_part(at * 2 + core, part)
            arrived(away, piece, qy_s.at[at, step], qy_r.at[at, step], partner)
            q_to_partner(away, at, part, piece)
        for at in range(chips):
            for row in range(seqs):
                away = jnp.logical_or(chip != at, place != row)
                piece = o_part(at * 2 + core, row, part)
                arrived(away, piece, oy_s.at[at, row, step], oy_r.at[at, row, step], partner)
                o_to_partner(away, at, row, part, piece)

    for at in range(chips):
        for part in range(groups):
            arrived(None, q_part(at * 2 + other, part), qc_s.at[at, part], qc_r.at[at, part], partner)
            for row in range(seqs):
                arrived(None, o_part(at * 2 + other, row, part), oc_s.at[at, row, part], oc_r.at[at, row, part], partner)
    for cond, made in sent:
        run(cond, lambda made=made: copy(*made).wait_send())
    for store in stores:
        store.wait()


def gather(norm, wq, wo):
    groups, tiles, seqs = (lax.axis_size(name) for name in ("group", "tile", "seq"))
    chips = tiles // 2
    pairs = [(2, seqs), (2, seqs), (2, chips), (2, chips, seqs), (chips, groups), (chips, seqs, groups), (chips, groups), (chips, seqs, groups)]
    return pl.pallas_call(
        functools.partial(gather_kernel, groups, chips, seqs),
        out_shape=(
            jax.ShapeDtypeStruct((seqs,) + norm.shape, norm.dtype),
            jax.ShapeDtypeStruct((tiles,) + wq.shape, wq.dtype),
            jax.ShapeDtypeStruct((tiles, seqs) + wo.shape, wo.dtype),
        ),
        in_specs=[pl.BlockSpec(memory_space=pl.ANY)] * 3,
        out_specs=(pl.BlockSpec(memory_space=pl.ANY),) * 3,
        scratch_shapes=[pltpu.VMEM(a.shape, a.dtype) for a in (norm, wq, wo)]
        + [pltpu.SemaphoreType.DMA((3,))]
        + [pltpu.SemaphoreType.DMA(shape) for shape in pairs for _ in range(2)],
        compiler_params=pltpu.CompilerParams(collective_id=0, has_side_effects=True),
    )(norm, wq, wo)


def shards(hidden, modulation, w_qkv, w_out, w_head, latent, weights_int, step_index):
    local = hidden[0].astype(jnp.float32)
    norm_in = (layer_norm(local) * (1.0 + modulation[1]) + modulation[0]).astype(jnp.bfloat16)
    rows, columns, out_blocks = gather(norm_in, w_qkv, w_out)
    gathered = rows.reshape(-1, rows.shape[2])
    length = gathered.shape[0]
    heads_here = w_qkv.shape[1] // (3 * HD)
    projected = jnp.dot(
        gathered, columns.reshape(-1, columns.shape[2]), preferred_element_type=jnp.float32
    )
    projected = projected.reshape(length, heads_here, 3, HD)
    queries = root_norm(projected[:, :, 0]).astype(jnp.bfloat16)
    keys = root_norm(projected[:, :, 1]).astype(jnp.bfloat16)
    values = projected[:, :, 2].astype(jnp.bfloat16)
    block = min(512, length)
    scale = 1.0 / math.sqrt(HD)
    pieces = []
    for first in range(0, length, block):
        scores = (
            jnp.einsum(
                "qhe,khe->hqk",
                queries[first : first + block],
                keys,
                preferred_element_type=jnp.float32,
            )
            * scale
        )
        expo = jnp.exp(scores)
        probs = (expo / jnp.sum(expo, axis=-1, keepdims=True)).astype(jnp.bfloat16)
        pieces.append(
            jnp.einsum("hqk,khe->qhe", probs, values, preferred_element_type=jnp.float32).astype(
                jnp.bfloat16
            )
        )
    attended = jnp.concatenate(pieces, axis=0).reshape(length, heads_here * HD)
    attended = lax.all_to_all(attended, "seq", split_axis=0, concat_axis=1, tiled=True)
    out_blocks = out_blocks.reshape(out_blocks.shape[0], -1, out_blocks.shape[3])
    summed = jnp.concatenate(
        [
            jnp.dot(attended, out_blocks[at], preferred_element_type=jnp.float32)
            for at in range(out_blocks.shape[0])
        ],
        axis=1,
    )
    mixed = local + modulation[2] * summed
    norm_out = (layer_norm(mixed) * (1.0 + modulation[4]) + modulation[3]).astype(jnp.bfloat16)
    velocity = jnp.dot(norm_out, w_head, preferred_element_type=jnp.float32)
    index = step_index[0].astype(jnp.float32)
    now = noise_level(index, NSTEPS)
    after = noise_level(index + 1.0, NSTEPS)
    base = latent[0]
    weight = weights_int[0].astype(jnp.float32)
    moved = base + (after - now) * velocity
    guess = base - now * velocity
    weighted = jnp.concatenate([moved, guess], axis=1) * weight[:, None]
    seq_count, tile_count = lax.axis_size("seq"), lax.axis_size("tile")
    jump = seq_count - 2
    moves = [
        (t * seq_count + s, (t + 1) * seq_count + s - jump)
        for t in range(tile_count - 1)
        for s in range(jump, seq_count)
    ]
    moves = moves + [(there, here) for here, there in moves]
    other_sums = lax.ppermute(weighted.astype(jnp.bfloat16), ("tile", "seq"), moves)
    other_weight = lax.ppermute(weight.astype(jnp.bfloat16), ("tile", "seq"), moves)
    totals = weighted + other_sums.astype(jnp.float32)
    norms = weight + other_weight.astype(jnp.float32)
    joined = totals / norms[:, None]
    channels = velocity.shape[1]
    return (joined[None, :, :channels], joined[None, :, channels:])


def solution(mesh):
    in_specs = (
        P(("group", "tile"), "seq", None),
        P("group", None),
        P("tile", "seq"),
        P("seq", "tile"),
        P(),
        P(("group", "tile"), "seq", None),
        P(("group", "tile"), "seq"),
        P("group"),
    )
    out_specs = (P(("group", "tile"), "seq", None), P(("group", "tile"), "seq", None))
    return jax.shard_map(shards, mesh=mesh, in_specs=in_specs, out_specs=out_specs, check_vma=False)
```

```python
import functools
import math

import jax
import jax.numpy as jnp
from jax import lax
from jax.experimental import pallas as pl
from jax.experimental.pallas import tpu as pltpu
from jax.sharding import PartitionSpec as P

HD = 128
NSTEPS = 28


def layer_norm(values):
    mean = jnp.mean(values, axis=-1, keepdims=True)
    centred = values - mean
    spread = jnp.mean(centred * centred, axis=-1, keepdims=True)
    return centred * lax.rsqrt(spread + 1e-06)


def root_norm(values):
    return values * lax.rsqrt(jnp.mean(values * values, axis=-1, keepdims=True) + 1e-06)


def noise_level(index, steps):
    level = 1.0 - index / steps
    return 3.0 * level / (1.0 + 2.0 * level)


MESH = pl.DeviceIdType.MESH


def run(cond, body):
    if cond is None:
        body()
    else:
        pl.when(cond)(body)


def arrives(place, count, way, far):
    return place >= far if way == 0 else place <= count - 1 - far


def goes_on(place, count, way):
    return place < count - 1 if way == 0 else place > 0


def gather_kernel(
    groups, chips, seqs, norm, wq, wo, n_all, q_all, o_all, v_norm, v_wq, v_wo, local,
    nz_s, nz_r, oz_s, oz_r, qx_s, qx_r, ox_s, ox_r, qy_s, qy_r, oy_s, oy_r, qc_s, qc_r, oc_s, oc_r,
):
    group, tile, place = lax.axis_index("group"), lax.axis_index("tile"), lax.axis_index("seq")
    chip, core = tile // 2, tile % 2
    other = 1 - core
    partner = {"tile": chip * 2 + other}
    q_rows, o_rows = wq.shape[0] // groups, wo.shape[0] // groups
    both = jnp.logical_and

    def q_part(owner, part):
        return q_all.at[owner, pl.ds(pl.multiple_of(part * q_rows, 8), q_rows)]

    def o_part(owner, row, part):
        return o_all.at[owner, row, pl.ds(pl.multiple_of(part * o_rows, 8), o_rows)]

    def along_seq(way):
        return {"seq": place + 1 - 2 * way}

    def along_chip(way):
        return {"tile": tile + 2 - 4 * way}

    def peer(step):
        return {"group": (group + step) % groups}

    barrier = pltpu.get_barrier_semaphore()
    greet = [(goes_on(place, seqs, way), along_seq(way)) for way in (0, 1)]
    greet += [(goes_on(chip, chips, way), along_chip(way)) for way in (0, 1)]
    greet += [(None, peer(step)) for step in range(1, groups)] + [(None, partner)]
    for cond, device in greet:
        run(cond, lambda device=device: pl.semaphore_signal(barrier, inc=1, device_id=device, device_id_type=MESH))
    met = groups + sum(goes_on(at, count, way).astype(jnp.int32) for at, count in ((place, seqs), (chip, chips)) for way in (0, 1))
    pl.semaphore_wait(barrier, met)

    sent = []

    def copy(source, target, send, recv, device):
        return pltpu.make_async_remote_copy(
            src_ref=source, dst_ref=target, send_sem=send, recv_sem=recv, device_id=device, device_id_type=MESH
        )

    def start(cond, *made):
        run(cond, lambda: copy(*made).start())
        sent.append((cond, made))

    def arrived(cond, target, send, recv, device):
        run(cond, lambda: copy(target, target, send, recv, device).wait_recv())

    def q_to_peers(cond, at, source):
        for step in range(1, groups):
            start(cond, source, q_part(at * 2 + core, group), qy_s.at[at, step], qy_r.at[at, step], peer(step))

    def q_to_partner(cond, at, part, source):
        start(cond, source, q_part(at * 2 + core, part), qc_s.at[at, part], qc_r.at[at, part], partner)

    def o_to_peers(cond, at, row, source):
        for step in range(1, groups):
            start(cond, source, o_part(at * 2 + core, row, group), oy_s.at[at, row, step], oy_r.at[at, row, step], peer(step))

    def o_to_partner(cond, at, row, part, source):
        start(cond, source, o_part(at * 2 + core, row, part), oc_s.at[at, row, part], oc_r.at[at, row, part], partner)

    def o_along_chip(cond, way, far, at, row, source):
        start(cond, source, o_part(at * 2 + core, row, group), ox_s.at[way, far, row], ox_r.at[way, far, row], along_chip(way))

    loads = [pltpu.make_async_copy(a, b, local.at[k]) for k, (a, b) in enumerate(((norm, v_norm), (wq, v_wq), (wo, v_wo)))]
    for load in loads:
        load.start()

    own_q = wq.at[pl.ds(pl.multiple_of(group * q_rows, 8), q_rows)]
    own_o = wo.at[pl.ds(pl.multiple_of(group * o_rows, 8), o_rows)]
    for way in (0, 1):
        go = goes_on(place, seqs, way)
        start(go, own_o, o_part(tile, place, group), oz_s.at[way, 1], oz_r.at[way, 1], along_seq(way))
        start(go, norm, n_all.at[place], nz_s.at[way, 1], nz_r.at[way, 1], along_seq(way))
        go = goes_on(chip, chips, way)
        start(go, own_q, q_part(tile, group), qx_s.at[way, 1], qx_r.at[way, 1], along_chip(way))
        o_along_chip(go, way, 1, chip, place, own_o)
    for part in range(groups):
        q_to_partner(None, chip, part, wq.at[pl.ds(part * q_rows, q_rows)])
        o_to_partner(None, chip, place, part, wo.at[pl.ds(part * o_rows, o_rows)])

    stores = [pltpu.make_async_copy(b, a, local.at[k]) for k, (a, b) in enumerate(((n_all.at[place], v_norm), (q_all.at[tile], v_wq), (o_all.at[tile, place], v_wo)))]
    for load in loads:
        load.wait()
    for store in stores:
        store.start()

    def rows_from_chips(rows):
        for far in range(1, chips):
            for way in (0, 1):
                at = chip - far if way == 0 else chip + far
                for given, row in rows:
                    here = arrives(chip, chips, way, far)
                    here = here if given is None else both(here, given)
                    piece = o_part(at * 2 + core, row, group)
                    arrived(here, piece, ox_s.at[way, far, row], ox_r.at[way, far, row], along_chip(way))
                    if far < chips - 1:
                        o_along_chip(both(here, goes_on(chip, chips, way)), way, far + 1, at, row, piece)
                    o_to_peers(here, at, row, piece)
                    o_to_partner(here, at, row, group, piece)

    def rows_at(far):
        if far == 0:
            return [(None, place)]
        return [(arrives(place, seqs, way, far), place - far if way == 0 else place + far) for way in (0, 1)]

    def seq_step(far):
        for way in (0, 1):
            here = arrives(place, seqs, way, far)
            row = place - far if way == 0 else place + far
            piece = o_part(tile, row, group)
            arrived(here, piece, oz_s.at[way, far], oz_r.at[way, far], along_seq(way))
            if far < seqs - 1:
                start(both(here, goes_on(place, seqs, way)), piece, piece, oz_s.at[way, far + 1], oz_r.at[way, far + 1], along_seq(way))
            for side in (0, 1):
                o_along_chip(both(here, goes_on(chip, chips, side)), side, 1, chip, row, piece)
            o_to_peers(here, chip, row, piece)
            o_to_partner(here, chip, row, group, piece)
        if far > 1:
            rows_from_chips(rows_at(far - 1))
        for way in (0, 1):
            here = arrives(place, seqs, way, far)
            row = place - far if way == 0 else place + far
            piece = n_all.at[row]
            arrived(here, piece, nz_s.at[way, far], nz_r.at[way, far], along_seq(way))
            if far < seqs - 1:
                start(both(here, goes_on(place, seqs, way)), piece, piece, nz_s.at[way, far + 1], nz_r.at[way, far + 1], along_seq(way))

    def chip_step(far):
        for way in (0, 1):
            here = arrives(chip, chips, way, far)
            at = chip - far if way == 0 else chip + far
            piece = q_part(at * 2 + core, group)
            arrived(here, piece, qx_s.at[way, far], qx_r.at[way, far], along_chip(way))
            if far < chips - 1:
                start(both(here, goes_on(chip, chips, way)), piece, piece, qx_s.at[way, far + 1], qx_r.at[way, far + 1], along_chip(way))
            q_to_peers(here, at, piece)
            q_to_partner(here, at, group, piece)

    for far in range(1, max(chips, seqs)):
        if far < seqs:
            seq_step(far)
        if far < chips:
            chip_step(far)
        if far == 1:
            rows_from_chips(rows_at(0))
    if seqs > 1:
        rows_from_chips(rows_at(seqs - 1))

    for step in range(1, groups):
        part = (group + groups - step) % groups
        for at in range(chips):
            away = chip != at
            piece = q_part(at * 2 + core, part)
            arrived(away, piece, qy_s.at[at, step], qy_r.at[at, step], partner)
            q_to_partner(away, at, part, piece)
        for at in range(chips):
            for row in range(seqs):
                away = jnp.logical_or(chip != at, place != row)
                piece = o_part(at * 2 + core, row, part)
                arrived(away, piece, oy_s.at[at, row, step], oy_r.at[at, row, step], partner)
                o_to_partner(away, at, row, part, piece)

    for at in range(chips):
        for part in range(groups):
            arrived(None, q_part(at * 2 + other, part), qc_s.at[at, part], qc_r.at[at, part], partner)
            for row in range(seqs):
                arrived(None, o_part(at * 2 + other, row, part), oc_s.at[at, row, part], oc_r.at[at, row, part], partner)
    for cond, made in sent:
        run(cond, lambda made=made: copy(*made).wait_send())
    for store in stores:
        store.wait()


def gather(norm, wq, wo):
    groups, tiles, seqs = (lax.axis_size(name) for name in ("group", "tile", "seq"))
    chips = tiles // 2
    pairs = [(2, seqs), (2, seqs), (2, chips), (2, chips, seqs), (chips, groups), (chips, seqs, groups), (chips, groups), (chips, seqs, groups)]
    return pl.pallas_call(
        functools.partial(gather_kernel, groups, chips, seqs),
        out_shape=(
            jax.ShapeDtypeStruct((seqs,) + norm.shape, norm.dtype),
            jax.ShapeDtypeStruct((tiles,) + wq.shape, wq.dtype),
            jax.ShapeDtypeStruct((tiles, seqs) + wo.shape, wo.dtype),
        ),
        in_specs=[pl.BlockSpec(memory_space=pl.ANY)] * 3,
        out_specs=(pl.BlockSpec(memory_space=pl.ANY),) * 3,
        scratch_shapes=[pltpu.VMEM(a.shape, a.dtype) for a in (norm, wq, wo)]
        + [pltpu.SemaphoreType.DMA((3,))]
        + [pltpu.SemaphoreType.DMA(shape) for shape in pairs for _ in range(2)],
        compiler_params=pltpu.CompilerParams(collective_id=0, has_side_effects=True),
    )(norm, wq, wo)


def heads_kernel(scale, block, rows, weights, attended, queries, keys, values):
    length = rows.shape[0]
    for first in range(0, length, block):
        at = pl.ds(first, block)
        part = jnp.dot(rows[at, :], weights[...], preferred_element_type=jnp.float32)
        queries[at, :] = root_norm(part[:, :HD]).astype(jnp.bfloat16)
        keys[at, :] = root_norm(part[:, HD : 2 * HD]).astype(jnp.bfloat16)
        values[at, :] = part[:, 2 * HD :].astype(jnp.bfloat16)
    for first in range(0, length, block):
        at = pl.ds(first, block)
        scores = lax.dot_general(
            queries[at, :], keys[...], (((1,), (1,)), ((), ())), preferred_element_type=jnp.float32
        )
        expo = jnp.exp(scores * scale)
        probs = (expo * (1.0 / jnp.sum(expo, axis=-1, keepdims=True))).astype(jnp.bfloat16)
        attended[at, :] = jnp.dot(probs, values[...], preferred_element_type=jnp.float32).astype(jnp.bfloat16)


def attend(rows, weights):
    length, width = rows.shape
    heads = weights.shape[1] // (3 * HD)
    return pl.pallas_call(
        functools.partial(heads_kernel, 1.0 / math.sqrt(HD), min(256, length)),
        grid=(heads,),
        out_shape=jax.ShapeDtypeStruct((length, heads * HD), jnp.bfloat16),
        in_specs=[
            pl.BlockSpec((length, width), lambda head: (0, 0), pipeline_mode=pl.Buffered(1)),
            pl.BlockSpec((width, 3 * HD), lambda head: (0, head)),
        ],
        out_specs=pl.BlockSpec((length, HD), lambda head: (0, head)),
        scratch_shapes=[pltpu.VMEM((length, HD), jnp.bfloat16)] * 3,
    )(rows, weights)


def tail_kernel(attended, blocks, hidden, modulation, w_head, velocity, summed):
    at = pl.program_id(0)
    width = blocks.shape[2]
    here = pl.ds(pl.multiple_of(at * width, 128), width)
    summed[:, here] = jnp.dot(attended[...], blocks[0], preferred_element_type=jnp.float32)

    @pl.when(at == pl.num_programs(0) - 1)
    def _():
        mixed = hidden[...].astype(jnp.float32) + modulation[2:3] * summed[...]
        norm_out = (layer_norm(mixed) * (1.0 + modulation[4:5]) + modulation[3:4]).astype(jnp.bfloat16)
        velocity[...] = jnp.dot(norm_out, w_head[...], preferred_element_type=jnp.float32)


def tail(attended, blocks, hidden, modulation, w_head):
    tiles, depth, width = blocks.shape
    if width % 128:
        summed = jnp.concatenate(
            [jnp.dot(attended, blocks[at], preferred_element_type=jnp.float32) for at in range(tiles)], axis=1
        )
        mixed = hidden.astype(jnp.float32) + modulation[2] * summed
        norm_out = (layer_norm(mixed) * (1.0 + modulation[4]) + modulation[3]).astype(jnp.bfloat16)
        return jnp.dot(norm_out, w_head, preferred_element_type=jnp.float32)
    whole = [pl.BlockSpec(a.shape, lambda at: (0, 0), pipeline_mode=pl.Buffered(1)) for a in (attended, hidden, modulation, w_head)]
    return pl.pallas_call(
        tail_kernel,
        grid=(tiles,),
        out_shape=jax.ShapeDtypeStruct((hidden.shape[0], w_head.shape[1]), jnp.float32),
        in_specs=[whole[0], pl.BlockSpec((1, depth, width), lambda at: (at, 0, 0)), *whole[1:]],
        out_specs=pl.BlockSpec((hidden.shape[0], w_head.shape[1]), lambda at: (0, 0)),
        scratch_shapes=[pltpu.VMEM(hidden.shape, jnp.float32)],
    )(attended, blocks, hidden, modulation, w_head)


def shards(hidden, modulation, w_qkv, w_out, w_head, latent, weights_int, step_index):
    local = hidden[0].astype(jnp.float32)
    norm_in = (layer_norm(local) * (1.0 + modulation[1]) + modulation[0]).astype(jnp.bfloat16)
    rows, columns, out_blocks = gather(norm_in, w_qkv, w_out)
    attended = attend(rows.reshape(-1, rows.shape[2]), columns.reshape(-1, columns.shape[2]))
    attended = lax.all_to_all(attended, "seq", split_axis=0, concat_axis=1, tiled=True)
    out_blocks = out_blocks.reshape(out_blocks.shape[0], -1, out_blocks.shape[3])
    velocity = tail(attended, out_blocks, hidden[0], modulation, w_head)
    index = step_index[0].astype(jnp.float32)
    now = noise_level(index, NSTEPS)
    after = noise_level(index + 1.0, NSTEPS)
    base = latent[0]
    weight = weights_int[0].astype(jnp.float32)
    moved = base + (after - now) * velocity
    guess = base - now * velocity
    weighted = jnp.concatenate([moved, guess], axis=1) * weight[:, None]
    seq_count, tile_count = lax.axis_size("seq"), lax.axis_size("tile")
    jump = seq_count - 2
    moves = [
        (t * seq_count + s, (t + 1) * seq_count + s - jump)
        for t in range(tile_count - 1)
        for s in range(jump, seq_count)
    ]
    moves = moves + [(there, here) for here, there in moves]
    other_sums = lax.ppermute(weighted.astype(jnp.bfloat16), ("tile", "seq"), moves)
    other_weight = lax.ppermute(weight.astype(jnp.bfloat16), ("tile", "seq"), moves)
    totals = weighted + other_sums.astype(jnp.float32)
    norms = weight + other_weight.astype(jnp.float32)
    joined = totals / norms[:, None]
    channels = velocity.shape[1]
    return (joined[None, :, :channels], joined[None, :, channels:])


def solution(mesh):
    in_specs = (
        P(("group", "tile"), "seq", None),
        P("group", None),
        P("tile", "seq"),
        P("seq", "tile"),
        P(),
        P(("group", "tile"), "seq", None),
        P(("group", "tile"), "seq"),
        P("group"),
    )
    out_specs = (P(("group", "tile"), "seq", None), P(("group", "tile"), "seq", None))
    return jax.shard_map(shards, mesh=mesh, in_specs=in_specs, out_specs=out_specs, check_vma=False)
```

```python
import functools
import math

import jax
import jax.numpy as jnp
from jax import lax
from jax.experimental import pallas as pl
from jax.experimental.pallas import tpu as pltpu
from jax.sharding import PartitionSpec as P

HD = 128
NSTEPS = 28


def layer_norm(values):
    mean = jnp.mean(values, axis=-1, keepdims=True)
    centred = values - mean
    spread = jnp.mean(centred * centred, axis=-1, keepdims=True)
    return centred * lax.rsqrt(spread + 1e-06)


def root_norm(values):
    return values * lax.rsqrt(jnp.mean(values * values, axis=-1, keepdims=True) + 1e-06)


def noise_level(index, steps):
    level = 1.0 - index / steps
    return 3.0 * level / (1.0 + 2.0 * level)


MESH = pl.DeviceIdType.MESH


def run(cond, body):
    if cond is None:
        body()
    else:
        pl.when(cond)(body)


def arrives(place, count, way, far):
    return place >= far if way == 0 else place <= count - 1 - far


def goes_on(place, count, way):
    return place < count - 1 if way == 0 else place > 0


def gather_kernel(
    groups, chips, seqs, scale, norm, wq, wo, q_all, o_all, attended,
    n_all, v_wq, v_wo, w_head, queries, keys, values, local, w_sem,
    nz_s, nz_r, oz_s, oz_r, qx_s, qx_r, ox_s, ox_r, qy_s, qy_r, oy_s, oy_r, qc_s, qc_r, oc_s, oc_r,
):
    group, tile, place = lax.axis_index("group"), lax.axis_index("tile"), lax.axis_index("seq")
    chip, core = tile // 2, tile % 2
    other = 1 - core
    partner = {"tile": chip * 2 + other}
    q_rows, o_rows = wq.shape[0] // groups, wo.shape[0] // groups
    both = jnp.logical_and

    def q_part(owner, part):
        return q_all.at[owner, pl.ds(pl.multiple_of(part * q_rows, 8), q_rows)]

    def o_part(owner, row, part):
        return o_all.at[owner, row, pl.ds(pl.multiple_of(part * o_rows, 8), o_rows)]

    def along_seq(way):
        return {"seq": place + 1 - 2 * way}

    def along_chip(way):
        return {"tile": tile + 2 - 4 * way}

    def peer(step):
        return {"group": (group + step) % groups}

    barrier = pltpu.get_barrier_semaphore()
    greet = [(goes_on(place, seqs, way), along_seq(way)) for way in (0, 1)]
    greet += [(goes_on(chip, chips, way), along_chip(way)) for way in (0, 1)]
    greet += [(None, peer(step)) for step in range(1, groups)] + [(None, partner)]
    for cond, device in greet:
        run(cond, lambda device=device: pl.semaphore_signal(barrier, inc=1, device_id=device, device_id_type=MESH))
    met = groups + sum(goes_on(at, count, way).astype(jnp.int32) for at, count in ((place, seqs), (chip, chips)) for way in (0, 1))
    pl.semaphore_wait(barrier, met)

    sent = []

    def copy(source, target, send, recv, device):
        return pltpu.make_async_remote_copy(
            src_ref=source, dst_ref=target, send_sem=send, recv_sem=recv, device_id=device, device_id_type=MESH
        )

    def start(cond, *made):
        run(cond, lambda: copy(*made).start())
        sent.append((cond, made))

    def arrived(cond, target, send, recv, device):
        run(cond, lambda: copy(target, target, send, recv, device).wait_recv())

    def q_to_peers(cond, at, source):
        for step in range(1, groups):
            start(cond, source, q_part(at * 2 + core, group), qy_s.at[at, step], qy_r.at[at, step], peer(step))

    def q_to_partner(cond, at, part, source):
        start(cond, source, q_part(at * 2 + core, part), qc_s.at[at, part], qc_r.at[at, part], partner)

    def o_to_peers(cond, at, row, source):
        for step in range(1, groups):
            start(cond, source, o_part(at * 2 + core, row, group), oy_s.at[at, row, step], oy_r.at[at, row, step], peer(step))

    def o_to_partner(cond, at, row, part, source):
        start(cond, source, o_part(at * 2 + core, row, part), oc_s.at[at, row, part], oc_r.at[at, row, part], partner)

    def o_along_chip(cond, way, far, at, row, source):
        start(cond, source, o_part(at * 2 + core, row, group), ox_s.at[way, far, row], ox_r.at[way, far, row], along_chip(way))

    loads = [pltpu.make_async_copy(a, b, local.at[k]) for k, (a, b) in enumerate(((norm, n_all.at[place]), (wq, v_wq), (wo, v_wo)))]
    for load in loads:
        load.start()

    own_q = wq.at[pl.ds(pl.multiple_of(group * q_rows, 8), q_rows)]
    own_o = wo.at[pl.ds(pl.multiple_of(group * o_rows, 8), o_rows)]
    for way in (0, 1):
        go = goes_on(place, seqs, way)
        start(go, norm, n_all.at[place], nz_s.at[way, 1], nz_r.at[way, 1], along_seq(way))
        start(go, own_o, o_part(tile, place, group), oz_s.at[way, 1], oz_r.at[way, 1], along_seq(way))
        go = goes_on(chip, chips, way)
        start(go, own_q, q_part(tile, group), qx_s.at[way, 1], qx_r.at[way, 1], along_chip(way))
        o_along_chip(go, way, 1, chip, place, own_o)
    for part in range(groups):
        q_to_partner(None, chip, part, wq.at[pl.ds(part * q_rows, q_rows)])
        o_to_partner(None, chip, place, part, wo.at[pl.ds(part * o_rows, o_rows)])

    stores = [pltpu.make_async_copy(b, a, local.at[k]) for k, (a, b) in enumerate(((q_all.at[tile], v_wq), (o_all.at[tile, place], v_wo)))]
    for load in loads:
        load.wait()
    for store in stores:
        store.start()

    def rows_from_chips(rows):
        for far in range(1, chips):
            for way in (0, 1):
                at = chip - far if way == 0 else chip + far
                for given, row in rows:
                    here = arrives(chip, chips, way, far)
                    here = here if given is None else both(here, given)
                    piece = o_part(at * 2 + core, row, group)
                    arrived(here, piece, ox_s.at[way, far, row], ox_r.at[way, far, row], along_chip(way))
                    if far < chips - 1:
                        o_along_chip(both(here, goes_on(chip, chips, way)), way, far + 1, at, row, piece)
                    o_to_peers(here, at, row, piece)
                    o_to_partner(here, at, row, group, piece)

    def rows_at(far):
        if far == 0:
            return [(None, place)]
        return [(arrives(place, seqs, way, far), place - far if way == 0 else place + far) for way in (0, 1)]

    def out_step(far):
        for way in (0, 1):
            here = arrives(place, seqs, way, far)
            row = place - far if way == 0 else place + far
            piece = o_part(tile, row, group)
            arrived(here, piece, oz_s.at[way, far], oz_r.at[way, far], along_seq(way))
            if far < seqs - 1:
                start(both(here, goes_on(place, seqs, way)), piece, piece, oz_s.at[way, far + 1], oz_r.at[way, far + 1], along_seq(way))
            for side in (0, 1):
                o_along_chip(both(here, goes_on(chip, chips, side)), side, 1, chip, row, piece)
            o_to_peers(here, chip, row, piece)
            o_to_partner(here, chip, row, group, piece)

    def norm_step(far):
        for way in (0, 1):
            here = arrives(place, seqs, way, far)
            row = place - far if way == 0 else place + far
            piece = n_all.at[row]
            arrived(here, piece, nz_s.at[way, far], nz_r.at[way, far], along_seq(way))
            if far < seqs - 1:
                start(both(here, goes_on(place, seqs, way)), piece, piece, nz_s.at[way, far + 1], nz_r.at[way, far + 1], along_seq(way))

    def chip_step(far):
        for way in (0, 1):
            here = arrives(chip, chips, way, far)
            at = chip - far if way == 0 else chip + far
            piece = q_part(at * 2 + core, group)
            arrived(here, piece, qx_s.at[way, far], qx_r.at[way, far], along_chip(way))
            if far < chips - 1:
                start(both(here, goes_on(chip, chips, way)), piece, piece, qx_s.at[way, far + 1], qx_r.at[way, far + 1], along_chip(way))
            q_to_peers(here, at, piece)
            q_to_partner(here, at, group, piece)

    def q_from_peers():
        for step in range(1, groups):
            part = (group + groups - step) % groups
            for at in range(chips):
                away = chip != at
                piece = q_part(at * 2 + core, part)
                arrived(away, piece, qy_s.at[at, step], qy_r.at[at, step], partner)
                q_to_partner(away, at, part, piece)

    def o_from_peers():
        for step in range(1, groups):
            part = (group + groups - step) % groups
            for at in range(chips):
                for row in range(seqs):
                    away = jnp.logical_or(chip != at, place != row)
                    piece = o_part(at * 2 + core, row, part)
                    arrived(away, piece, oy_s.at[at, row, step], oy_r.at[at, row, step], partner)
                    o_to_partner(away, at, row, part, piece)

    last = max(chips, seqs) - 1
    for far in range(1, last + 1):
        if 1 < far < seqs:
            rows_from_chips(rows_at(far - 1))
        if far < seqs:
            norm_step(far)
        if far < seqs - 1:
            out_step(far)
        if far < chips:
            chip_step(far)
        if far == 1 and seqs > 1:
            rows_from_chips(rows_at(0))
        if far == max(chips - 1, min(2, last)):
            q_from_peers()
    for at in range(chips):
        for part in range(groups):
            arrived(None, q_part(at * 2 + other, part), qc_s.at[at, part], qc_r.at[at, part], partner)
    for store in stores:
        store.wait()

    heads = wq.shape[1] // (3 * HD)
    depth, block = wq.shape[0], norm.shape[0]

    def fetch(head):
        slot = head % 2
        columns = pl.ds(pl.multiple_of(head * (3 * HD), 128), 3 * HD)
        return [
            pltpu.make_async_copy(
                q_all.at[at, :, columns], w_head.at[slot, pl.ds(at * depth, depth)], w_sem.at[slot, at]
            )
            for at in range(2 * chips)
        ]

    def one_head(head, carry):
        for load in fetch(head):
            load.wait()

        @pl.when(head + 1 < heads)
        def _():
            for load in fetch(head + 1):
                load.start()

        weights = w_head.at[head % 2]
        for row in range(seqs):
            at = pl.ds(row * block, block)
            part = jnp.dot(n_all[row], weights[...], preferred_element_type=jnp.float32)
            queries[at, :] = root_norm(part[:, :HD]).astype(jnp.bfloat16)
            keys[at, :] = root_norm(part[:, HD : 2 * HD]).astype(jnp.bfloat16)
            values[at, :] = part[:, 2 * HD :].astype(jnp.bfloat16)
        for row in range(seqs):
            at = pl.ds(row * block, block)
            scores = lax.dot_general(
                queries[at, :], keys[...], (((1,), (1,)), ((), ())), preferred_element_type=jnp.float32
            )
            expo = jnp.exp(scores * scale)
            probs = (expo * (1.0 / jnp.sum(expo, axis=-1, keepdims=True))).astype(jnp.bfloat16)
            attended[at, pl.ds(pl.multiple_of(head * HD, 128), HD)] = jnp.dot(
                probs, values[...], preferred_element_type=jnp.float32
            ).astype(jnp.bfloat16)
        return carry

    def between(step):
        if step == 0 and seqs > 1:
            out_step(seqs - 1)
        if step == 1:
            rows_from_chips(rows_at(seqs - 1))
        if step == 2:
            o_from_peers()

    for load in fetch(0):
        load.start()
    cuts = [0, heads // 3, heads // 2, 5 * heads // 6, heads]
    for step in range(4):
        if cuts[step] < cuts[step + 1]:
            lax.fori_loop(cuts[step], cuts[step + 1], one_head, 0)
        between(step)

    for at in range(chips):
        for part in range(groups):
            for row in range(seqs):
                arrived(None, o_part(at * 2 + other, row, part), oc_s.at[at, row, part], oc_r.at[at, row, part], partner)
    for cond, made in sent:
        run(cond, lambda made=made: copy(*made).wait_send())


def gather(norm, wq, wo):
    groups, tiles, seqs = (lax.axis_size(name) for name in ("group", "tile", "seq"))
    chips = tiles // 2
    length = seqs * norm.shape[0]
    pairs = [(2, seqs), (2, seqs), (2, chips), (2, chips, seqs), (chips, groups), (chips, seqs, groups), (chips, groups), (chips, seqs, groups)]
    return pl.pallas_call(
        functools.partial(gather_kernel, groups, chips, seqs, 1.0 / math.sqrt(HD)),
        out_shape=(
            jax.ShapeDtypeStruct((tiles,) + wq.shape, wq.dtype),
            jax.ShapeDtypeStruct((tiles, seqs) + wo.shape, wo.dtype),
            jax.ShapeDtypeStruct((length, wq.shape[1] // 3), norm.dtype),
        ),
        in_specs=[pl.BlockSpec(memory_space=pl.ANY)] * 3,
        out_specs=(pl.BlockSpec(memory_space=pl.ANY),) * 2 + (pl.BlockSpec(memory_space=pltpu.VMEM),),
        scratch_shapes=[pltpu.VMEM((seqs,) + norm.shape, norm.dtype)]
        + [pltpu.VMEM(a.shape, a.dtype) for a in (wq, wo)]
        + [pltpu.VMEM((2, tiles * wq.shape[0], 3 * HD), wq.dtype)]
        + [pltpu.VMEM((length, HD), norm.dtype)] * 3
        + [pltpu.SemaphoreType.DMA((3,)), pltpu.SemaphoreType.DMA((2, tiles))]
        + [pltpu.SemaphoreType.DMA(shape) for shape in pairs for _ in range(2)],
        compiler_params=pltpu.CompilerParams(collective_id=0, has_side_effects=True),
    )(norm, wq, wo)


def tail_kernel(attended, blocks, hidden, modulation, w_head, velocity, summed):
    at = pl.program_id(0)
    width = blocks.shape[2]
    here = pl.ds(pl.multiple_of(at * width, 128), width)
    summed[:, here] = jnp.dot(attended[...], blocks[0], preferred_element_type=jnp.float32)

    @pl.when(at == pl.num_programs(0) - 1)
    def _():
        mixed = hidden[...].astype(jnp.float32) + modulation[2:3] * summed[...]
        norm_out = (layer_norm(mixed) * (1.0 + modulation[4:5]) + modulation[3:4]).astype(jnp.bfloat16)
        velocity[...] = jnp.dot(norm_out, w_head[...], preferred_element_type=jnp.float32)


def tail(attended, blocks, hidden, modulation, w_head):
    tiles, depth, width = blocks.shape
    if width % 128:
        summed = jnp.concatenate(
            [jnp.dot(attended, blocks[at], preferred_element_type=jnp.float32) for at in range(tiles)], axis=1
        )
        mixed = hidden.astype(jnp.float32) + modulation[2] * summed
        norm_out = (layer_norm(mixed) * (1.0 + modulation[4]) + modulation[3]).astype(jnp.bfloat16)
        return jnp.dot(norm_out, w_head, preferred_element_type=jnp.float32)
    whole = [pl.BlockSpec(a.shape, lambda at: (0, 0), pipeline_mode=pl.Buffered(1)) for a in (attended, hidden, modulation, w_head)]
    return pl.pallas_call(
        tail_kernel,
        grid=(tiles,),
        out_shape=jax.ShapeDtypeStruct((hidden.shape[0], w_head.shape[1]), jnp.float32),
        in_specs=[whole[0], pl.BlockSpec((1, depth, width), lambda at: (at, 0, 0)), *whole[1:]],
        out_specs=pl.BlockSpec((hidden.shape[0], w_head.shape[1]), lambda at: (0, 0)),
        scratch_shapes=[pltpu.VMEM(hidden.shape, jnp.float32)],
    )(attended, blocks, hidden, modulation, w_head)


def shards(hidden, modulation, w_qkv, w_out, w_head, latent, weights_int, step_index):
    local = hidden[0].astype(jnp.float32)
    norm_in = (layer_norm(local) * (1.0 + modulation[1]) + modulation[0]).astype(jnp.bfloat16)
    _, out_blocks, attended = gather(norm_in, w_qkv, w_out)
    attended = lax.all_to_all(attended, "seq", split_axis=0, concat_axis=1, tiled=True)
    out_blocks = out_blocks.reshape(out_blocks.shape[0], -1, out_blocks.shape[3])
    velocity = tail(attended, out_blocks, hidden[0], modulation, w_head)
    index = step_index[0].astype(jnp.float32)
    now = noise_level(index, NSTEPS)
    after = noise_level(index + 1.0, NSTEPS)
    base = latent[0]
    weight = weights_int[0].astype(jnp.float32)
    moved = base + (after - now) * velocity
    guess = base - now * velocity
    weighted = jnp.concatenate([moved, guess], axis=1) * weight[:, None]
    seq_count, tile_count = lax.axis_size("seq"), lax.axis_size("tile")
    jump = seq_count - 2
    moves = [
        (t * seq_count + s, (t + 1) * seq_count + s - jump)
        for t in range(tile_count - 1)
        for s in range(jump, seq_count)
    ]
    moves = moves + [(there, here) for here, there in moves]
    other_sums = lax.ppermute(weighted.astype(jnp.bfloat16), ("tile", "seq"), moves)
    other_weight = lax.ppermute(weight.astype(jnp.bfloat16), ("tile", "seq"), moves)
    totals = weighted + other_sums.astype(jnp.float32)
    norms = weight + other_weight.astype(jnp.float32)
    joined = totals / norms[:, None]
    channels = velocity.shape[1]
    return (joined[None, :, :channels], joined[None, :, channels:])


def solution(mesh):
    in_specs = (
        P(("group", "tile"), "seq", None),
        P("group", None),
        P("tile", "seq"),
        P("seq", "tile"),
        P(),
        P(("group", "tile"), "seq", None),
        P(("group", "tile"), "seq"),
        P("group"),
    )
    out_specs = (P(("group", "tile"), "seq", None), P(("group", "tile"), "seq", None))
    return jax.shard_map(shards, mesh=mesh, in_specs=in_specs, out_specs=out_specs, check_vma=False)
```
